32 devices in a mesh: tok: 8 (over y, x, core), lat: 4 (over z).
Axes of the slice: x: 2, y: 2, z: 4, core: 2. Of those that a mesh axis runs over, the one named last changes fastest.
Arguments:
- captured: bfloat16 [1024, 16384], P(None, 'tok'), may hold values from -6 to 6
- enc_weight: bfloat16 [16384, 16384], P('tok', 'lat'), may hold values from -0.046875 to 0.046875
- enc_bias: float32 [16384], P('lat'), may hold values from -3 to 3
- dec_weight: bfloat16 [16384, 16384], P('lat', 'tok'), may hold values from -0.1875 to 0.1875
- dec_bias: float32 [16384], P('tok'), may hold values from -1.5 to 1.5
- block_ids: int32 [8, 4, 2], P(None, 'lat'), may hold values from 0 to 31, as said below
- block_counts: int32 [8, 4], P(None, 'lat'), may hold values from 1 to 2, as said below
Outputs:
- enc_grad: bfloat16 [16384, 16384], P('tok', 'lat')
- dec_grad: bfloat16 [16384, 16384], P('lat', 'tok')
The draws below stay inside these ranges and needn't reach their ends.
Inputs may be any that keep to these rules, and one draw needn't show every extreme that they name: block_ids[b, s, k] numbers a latent block within latent shard s; the 2 entries of one token block and shard are distinct, and those with k >= block_counts[b, s] are inactive slots. block_counts[b, s] is how many leading slots of block_ids[b, s] are active; some entry equals 2 in every draw.
All inputs are finite; a program needn't handle non-finite values.
Results may differ from the reference program's by a relative error of at most 0.02.
Values may be sent and summed in bfloat16 or wider, within the bound.
A program may use at most 192 MiB of HBM per device.

```python
import jax
import jax.numpy as jnp
from jax import lax

L = 16384
TB = 128
LB = 128
KS = 2
F = 16384
TOKENS = 1024
NTB = 8
LBD = 32
ACTIVE = 1024
N_LAT = 4


def pick_row(row_key):
    return jax.random.permutation(row_key, LBD)[:KS]


def draw_block_ids(key, part):
    row_keys = jax.random.split(jax.random.fold_in(key, 11), NTB * N_LAT)
    chosen = jax.vmap(pick_row)(row_keys)
    return chosen.reshape(NTB, N_LAT, KS).astype(jnp.int32)


def draw_block_counts(key, part):
    base_key = jax.random.fold_in(key, 23)
    key_level, key_extra, key_row, key_col = jax.random.split(base_key, 4)
    levels = jax.random.randint(key_level, (N_LAT,), 0, KS)
    extra_slots = jax.random.randint(key_extra, (NTB, N_LAT), 0, KS)
    counts = 1 + jnp.minimum(extra_slots, levels[None, :])
    row_at = jax.random.randint(key_row, (), 0, NTB)
    col_at = jax.random.randint(key_col, (), 0, N_LAT)
    return counts.at[row_at, col_at].set(KS).astype(jnp.int32)


def level_of(key, shape, shards, least, high):
    def one(dim, parts):
        heights = jax.random.uniform(jax.random.fold_in(jax.random.fold_in(key, 6), dim), (parts,), jnp.float32, least / len(shards), high / len(shards))
        return jnp.repeat(jnp.exp(heights), shape[dim] // parts).reshape((-1,) + (1,) * (len(shape) - dim - 1))

    loudness = one(*shards[0])
    for cut in shards[1:]:
        loudness = loudness * one(*cut)
    return loudness


def bell_draw(key, shape, deviation, reach, shards=(), kind=jnp.bfloat16):
    level = level_of(key, shape, shards, -0.22, 0.18) if shards else 1.0
    drawn = jax.random.normal(key, shape, jnp.float32) * deviation * level
    return jnp.minimum(jnp.maximum(drawn, -reach), reach).astype(kind)


def setup_inputs(seed: int = 0) -> dict:
    streams_of = jax.random.split(jax.random.key(seed), 8)
    captured = bell_draw(streams_of[0], (TOKENS, F), 1.0, 6.0, ((1, 8),))
    enc_weight = bell_draw(streams_of[1], (F, L), F ** -0.5, 0.046875, ((0, 8), (1, 4)))
    enc_bias = bell_draw(streams_of[2], (L,), 0.5, 3.0, ((0, 4),), jnp.float32)
    dec_weight = bell_draw(streams_of[3], (L, F), ACTIVE ** -0.5, 0.1875, ((0, 4), (1, 8)))
    dec_bias = bell_draw(streams_of[4], (F,), 0.25, 1.5, ((0, 8),), jnp.float32)
    block_ids = draw_block_ids(jax.random.fold_in(streams_of[7], 71), 0)
    block_counts = draw_block_counts(jax.random.fold_in(streams_of[7], 71), 0)
    return dict(captured=captured, enc_weight=enc_weight, enc_bias=enc_bias, dec_weight=dec_weight, dec_bias=dec_bias, block_ids=block_ids, block_counts=block_counts)


SCALE_ERR = 0.0625
PENALTY = 0.05


def reference(captured, enc_weight, enc_bias, dec_weight, dec_bias, block_ids, block_counts):
    features = captured.shape[1]
    all_blocks = captured.shape[0] // TB
    lat_blocks = L // LB
    slots = N_LAT * KS
    enc_cube = enc_weight.reshape(features, lat_blocks, LB)
    dec_cube = dec_weight.reshape(lat_blocks, LB, features)
    bias_cube = enc_bias.reshape(lat_blocks, LB)
    offsets = (jnp.arange(N_LAT, dtype=jnp.int32) * LBD)[:, None]
    rows_all = captured.reshape(all_blocks, TB, features)

    def one_block(inputs):
        rows_in, ids_row, counts_row = inputs
        global_ids = (offsets + ids_row).reshape(slots).astype(jnp.int32)
        enc_tiles = jnp.take(enc_cube, global_ids, axis=1).astype(jnp.float32)
        pre_act = jnp.einsum("tf,fmc->mtc", rows_in.astype(jnp.float32), enc_tiles)
        pre_act = pre_act + jnp.take(bias_cube, global_ids, axis=0)[:, None, :]
        live_slots = (jnp.arange(KS, dtype=jnp.int32)[None, :] < counts_row[:, None]).reshape(slots)
        codes = (jax.nn.softplus(pre_act) * live_slots.astype(jnp.float32)[:, None, None]).astype(jnp.bfloat16)
        dec_tiles = jnp.take(dec_cube, global_ids, axis=0).astype(jnp.float32)
        partial_value = jnp.einsum("lktc,lkcf->ltf", codes.astype(jnp.float32).reshape(N_LAT, KS, TB, LB),
                             dec_tiles.reshape(N_LAT, KS, LB, features))
        partial_value = lax.optimization_barrier(partial_value.astype(jnp.bfloat16)).astype(jnp.float32)
        rebuilt = jnp.sum(partial_value, axis=0)
        err_grad = SCALE_ERR * (rebuilt + dec_bias[None, :] - rows_in.astype(jnp.float32))
        err_half = err_grad.astype(jnp.bfloat16)
        code_grads = jnp.einsum("tf,mcf->mtc", err_half.astype(jnp.float32), dec_tiles)
        pre_grads = ((code_grads + PENALTY) * (1.0 - jnp.exp(-codes.astype(jnp.float32)))).astype(jnp.bfloat16)
        return codes, err_half, pre_grads

    codes, err_half, pre_grads = lax.map(one_block, (rows_all, block_ids, block_counts))
    codes_shard = codes.reshape(all_blocks, N_LAT, KS, TB, LB).transpose(1, 0, 2, 3, 4)
    grads_shard = pre_grads.reshape(all_blocks, N_LAT, KS, TB, LB).transpose(1, 0, 2, 3, 4)
    ids_shard = block_ids.transpose(1, 0, 2)

    def one_shard(inputs):
        shard_codes, shard_grads, shard_ids = inputs

        def step(carry, item):
            dec_acc, enc_acc = carry
            code_tiles, grad_tiles, chosen, rows_in, err_rows = item
            tile_dec = jnp.einsum("ktc,tf->kcf", code_tiles.astype(jnp.float32), err_rows.astype(jnp.float32))
            tile_enc = jnp.einsum("tf,ktc->fkc", rows_in.astype(jnp.float32), grad_tiles.astype(jnp.float32))
            return (dec_acc.at[chosen].add(tile_dec), enc_acc.at[:, chosen].add(tile_enc)), None

        start_acc = (jnp.zeros((LBD, LB, features), jnp.float32), jnp.zeros((features, LBD, LB), jnp.float32))
        (dec_acc, enc_acc), unused = lax.scan(step, start_acc, (shard_codes, shard_grads, shard_ids, rows_all, err_half))
        return (dec_acc.reshape(LBD * LB, features).astype(jnp.bfloat16),
                enc_acc.reshape(features, LBD * LB).astype(jnp.bfloat16))

    dec_parts, enc_parts = lax.map(one_shard, (codes_shard, grads_shard, ids_shard))
    dec_grad = dec_parts.reshape(L, features)
    enc_grad = enc_parts.transpose(1, 0, 2).reshape(features, L)
    return enc_grad, dec_grad
```

```python
import functools

import jax
import jax.numpy as jnp
from jax import lax
from jax.experimental import pallas as pl
from jax.experimental.pallas import tpu as pltpu
from jax.sharding import PartitionSpec as P

TB = 128
LB = 128
KS = 2

SCALE_ERR = 0.0625
PENALTY = 0.05
F32 = jnp.float32
BF16 = jnp.bfloat16
MESH = pl.DeviceIdType.MESH
VMEM = pltpu.VMEM
BIG = 60 * 1024 * 1024


def dot(a, b, ca, cb):
    return lax.dot_general(a, b, (((ca,), (cb,)), ((), ())), preferred_element_type=F32)


def pre_kernel(ids, counts, cap_ref, enc_ref, bias_ref, pre_ref, bsel_ref, live_ref):
    i = pl.program_id(0)
    pre_ref[...] = dot(cap_ref[...], enc_ref[...], 1, 0).astype(BF16)
    bsel_ref[...] = bias_ref[...]
    on = (lax.rem(i, KS) < counts[i // KS]).astype(F32)
    live_ref[...] = jnp.full(live_ref.shape, on, F32)


def partial_pre(ids, counts, captured, enc_weight, enc_bias):
    features = captured.shape[1]
    slots = ids.shape[0]
    row = pl.BlockSpec((1, 1, LB), lambda i, ids, counts: (i, 0, 0))
    return pl.pallas_call(
        pre_kernel,
        grid_spec=pltpu.PrefetchScalarGridSpec(
            num_scalar_prefetch=2,
            grid=(slots,),
            in_specs=[
                pl.BlockSpec((TB, features), lambda i, ids, counts: (i // KS, 0)),
                pl.BlockSpec((features, LB), lambda i, ids, counts: (0, ids[i])),
                pl.BlockSpec((1, 1, LB), lambda i, ids, counts: (ids[i], 0, 0)),
            ],
            out_specs=[pl.BlockSpec((TB, LB), lambda i, ids, counts: (i, 0)), row, row],
        ),
        out_shape=[
            jax.ShapeDtypeStruct((slots * TB, LB), BF16),
            jax.ShapeDtypeStruct((slots, 1, LB), F32),
            jax.ShapeDtypeStruct((slots, 1, LB), F32),
        ],
        compiler_params=pltpu.CompilerParams(vmem_limit_bytes=BIG),
        name="partial_pre",
    )(ids, counts, captured, enc_weight, enc_bias.reshape(-1, 1, LB))


def exchange_kernel(n, finish, part_ref, *refs):
    *extra, out_ref, recv, send_sem, recv_sem, give_sem, got_sem = refs
    me = lax.axis_index("tok")
    barrier = pltpu.get_barrier_semaphore()
    for d in range(1, n):
        pl.semaphore_signal(barrier, inc=1, device_id={"tok": lax.rem(me + d, n)}, device_id_type=MESH)
    pl.semaphore_wait(barrier, n - 1)
    outgoing = []
    for d in range(1, n):
        peer = lax.rem(me + d, n)
        copy = pltpu.make_async_remote_copy(
            src_ref=part_ref.at[peer],
            dst_ref=recv.at[d - 1],
            send_sem=send_sem.at[d - 1],
            recv_sem=recv_sem.at[d - 1],
            device_id={"tok": peer},
            device_id_type=MESH,
        )
        copy.start()
        outgoing.append(copy)
    for copy in outgoing:
        copy.wait()
    total = part_ref[me].astype(F32)
    for d in range(1, n):
        total = total + recv[d - 1].astype(F32)
    out_ref[me] = finish(me, total, *extra)
    outgoing = []
    for d in range(1, n):
        copy = pltpu.make_async_remote_copy(
            src_ref=out_ref.at[me],
            dst_ref=out_ref.at[me],
            send_sem=give_sem.at[d - 1],
            recv_sem=got_sem.at[d - 1],
            device_id={"tok": lax.rem(me + d, n)},
            device_id_type=MESH,
        )
        copy.start()
        outgoing.append(copy)
    for copy in outgoing:
        copy.wait_send()
    for d in range(1, n):
        source = lax.rem(me + n - d, n)
        pltpu.make_async_remote_copy(
            src_ref=out_ref.at[source],
            dst_ref=out_ref.at[source],
            send_sem=give_sem.at[d - 1],
            recv_sem=got_sem.at[d - 1],
            device_id={"tok": source},
            device_id_type=MESH,
        ).wait_recv()


def exchange(finish, ident, name, part, *extra):
    n = lax.axis_size("tok")
    rows = part.shape[0] // n
    whole = pl.BlockSpec(memory_space=VMEM)
    out = pl.pallas_call(
        functools.partial(exchange_kernel, n, finish),
        out_shape=jax.ShapeDtypeStruct((n, rows, LB), BF16),
        in_specs=[whole] * (1 + len(extra)),
        out_specs=whole,
        scratch_shapes=[VMEM((n - 1, rows, LB), BF16)] + [pltpu.SemaphoreType.DMA((n - 1,))] * 4,
        compiler_params=pltpu.CompilerParams(
            collective_id=ident, has_side_effects=True, vmem_limit_bytes=BIG
        ),
        name=name,
    )(part.reshape(n, rows, LB), *extra)
    return out.reshape(n * rows, LB)


def make_codes(me, total, bias_ref, live_ref):
    slots = total.shape[0] // TB
    outs = []
    for s in range(slots):
        v = total[s * TB:(s + 1) * TB] + bias_ref[me * slots + s]
        soft = jnp.maximum(v, 0.0) + jnp.log1p(jnp.exp(-jnp.abs(v)))
        outs.append((soft * live_ref[me * slots + s]).astype(BF16))
    return jnp.concatenate(outs, axis=0)


def make_dpre(me, total, codes_ref):
    return ((total + PENALTY) * (1.0 - jnp.exp(-codes_ref[me].astype(F32)))).astype(BF16)


def part_kernel(ids, codes_ref, *refs):
    *dec_refs, out_ref = refs
    total = dot(codes_ref[0:TB], dec_refs[0][...], 1, 0)
    for k in range(1, KS):
        total = total + dot(codes_ref[k * TB:(k + 1) * TB], dec_refs[k][...], 1, 0)
    out_ref[...] = total.astype(BF16)


def dec_specs(features):
    return [
        pl.BlockSpec((LB, features), functools.partial(lambda k, b, ids: (ids[b * KS + k], 0), k))
        for k in range(KS)
    ]


def rebuild_part(ids, codes, dec_weight):
    features = dec_weight.shape[1]
    blocks = ids.shape[0] // KS
    return pl.pallas_call(
        part_kernel,
        grid_spec=pltpu.PrefetchScalarGridSpec(
            num_scalar_prefetch=1,
            grid=(blocks,),
            in_specs=[pl.BlockSpec((KS * TB, LB), lambda b, ids: (b, 0))] + dec_specs(features),
            out_specs=pl.BlockSpec((TB, features), lambda b, ids: (b, 0)),
        ),
        out_shape=jax.ShapeDtypeStruct((blocks * TB, features), BF16),
        compiler_params=pltpu.CompilerParams(vmem_limit_bytes=BIG),
        name="rebuild_part",
    )(ids, codes, *([dec_weight] * KS))


def line_kernel(
    n, chunk, lag, part_ref, cap_ref, bias_ref, out_ref, up_in, down_in, up_out, down_out,
    up_send, up_recv, down_send, down_recv,
):
    me = lax.axis_index("lat")
    chunks = part_ref.shape[0] // chunk
    has_low = me > 0
    has_high = me < n - 1
    low = jnp.maximum(me - 1, 0)
    high = jnp.minimum(me + 1, n - 1)
    barrier = pltpu.get_barrier_semaphore()

    @pl.when(has_low)
    def _():
        pl.semaphore_signal(barrier, inc=1, device_id={"lat": low}, device_id_type=MESH)

    @pl.when(has_high)
    def _():
        pl.semaphore_signal(barrier, inc=1, device_id={"lat": high}, device_id_type=MESH)

    pl.semaphore_wait(barrier, has_low.astype(jnp.int32) + has_high.astype(jnp.int32))

    def rows(c):
        return pl.ds(pl.multiple_of(c * chunk, chunk), chunk)

    def up(c):
        return pltpu.make_async_remote_copy(
            src_ref=up_out.at[rows(c)], dst_ref=up_in.at[rows(c)],
            send_sem=up_send.at[c], recv_sem=up_recv.at[c],
            device_id={"lat": high}, device_id_type=MESH,
        )

    def up_first(c):
        return pltpu.make_async_remote_copy(
            src_ref=part_ref.at[rows(c)], dst_ref=up_in.at[rows(c)],
            send_sem=up_send.at[c], recv_sem=up_recv.at[c],
            device_id={"lat": high}, device_id_type=MESH,
        )

    def down(c):
        return pltpu.make_async_remote_copy(
            src_ref=down_out.at[rows(c)], dst_ref=down_in.at[rows(c)],
            send_sem=down_send.at[c], recv_sem=down_recv.at[c],
            device_id={"lat": low}, device_id_type=MESH,
        )

    def down_first(c):
        return pltpu.make_async_remote_copy(
            src_ref=part_ref.at[rows(c)], dst_ref=down_in.at[rows(c)],
            send_sem=down_send.at[c], recv_sem=down_recv.at[c],
            device_id={"lat": low}, device_id_type=MESH,
        )

    up_delay = lag * me
    down_delay = lag * (n - 1 - me)
    last_delay = jnp.maximum(up_delay, down_delay)

    def step(i, carry):
        cu = i - up_delay
        cd = i - down_delay
        cl = i - last_delay

        @pl.when(jnp.logical_and(cu >= 0, cu < chunks))
        def _():
            @pl.when(has_low)
            def _():
                up(cu).wait_recv()

                @pl.when(has_high)
                def _():
                    up_out[rows(cu)] = (up_in[rows(cu)].astype(F32) + part_ref[rows(cu)].astype(F32)).astype(BF16)
                    up(cu).start()

            @pl.when(jnp.logical_not(has_low))
            def _():
                up_first(cu).start()

        @pl.when(jnp.logical_and(cd >= 0, cd < chunks))
        def _():
            @pl.when(has_high)
            def _():
                down(cd).wait_recv()

                @pl.when(has_low)
                def _():
                    down_out[rows(cd)] = (down_in[rows(cd)].astype(F32) + part_ref[rows(cd)].astype(F32)).astype(BF16)
                    down(cd).start()

            @pl.when(jnp.logical_not(has_high))
            def _():
                down_first(cd).start()

        @pl.when(jnp.logical_and(cl >= 0, cl < chunks))
        def _():
            own = part_ref[rows(cl)].astype(F32) + bias_ref[...] - cap_ref[rows(cl)].astype(F32)

            @pl.when(jnp.logical_and(has_low, has_high))
            def _():
                both = up_in[rows(cl)].astype(F32) + down_in[rows(cl)].astype(F32)
                out_ref[rows(cl)] = (SCALE_ERR * (own + both)).astype(BF16)

            @pl.when(jnp.logical_not(has_low))
            def _():
                out_ref[rows(cl)] = (SCALE_ERR * (own + down_in[rows(cl)].astype(F32))).astype(BF16)

            @pl.when(jnp.logical_not(has_high))
            def _():
                out_ref[rows(cl)] = (SCALE_ERR * (own + up_in[rows(cl)].astype(F32))).astype(BF16)

        return carry

    lax.fori_loop(0, chunks + lag * (n - 1), step, 0)

    def drain(c, carry):
        @pl.when(has_high)
        def _():
            up(c).wait_send()

        @pl.when(has_low)
        def _():
            down(c).wait_send()

        return carry

    lax.fori_loop(0, chunks, drain, 0)


def line_delta(part, captured, dec_bias, chunk, lag):
    n = lax.axis_size("lat")
    tokens, features = part.shape
    chunks = tokens // chunk
    whole = pl.BlockSpec(memory_space=VMEM)
    return pl.pallas_call(
        functools.partial(line_kernel, n, chunk, lag),
        out_shape=jax.ShapeDtypeStruct((tokens, features), BF16),
        in_specs=[whole] * 3,
        out_specs=whole,
        scratch_shapes=[VMEM((tokens, features), BF16)] * 4 + [pltpu.SemaphoreType.DMA((chunks,))] * 4,
        compiler_params=pltpu.CompilerParams(
            collective_id=1, has_side_effects=True, vmem_limit_bytes=BIG
        ),
        name="line_delta",
    )(part, captured, dec_bias.reshape(1, features))


def dcodes_kernel(ids, delta_ref, *refs):
    *dec_refs, out_ref = refs
    for k in range(KS):
        out_ref[k * TB:(k + 1) * TB] = dot(delta_ref[...], dec_refs[k][...], 1, 1).astype(BF16)


def partial_dcodes(ids, delta, dec_weight):
    features = dec_weight.shape[1]
    blocks = ids.shape[0] // KS
    return pl.pallas_call(
        dcodes_kernel,
        grid_spec=pltpu.PrefetchScalarGridSpec(
            num_scalar_prefetch=1,
            grid=(blocks,),
            in_specs=[pl.BlockSpec((TB, features), lambda b, ids: (b, 0))] + dec_specs(features),
            out_specs=pl.BlockSpec((KS * TB, LB), lambda b, ids: (b, 0)),
        ),
        out_shape=jax.ShapeDtypeStruct((blocks * KS * TB, LB), BF16),
        compiler_params=pltpu.CompilerParams(vmem_limit_bytes=BIG),
        name="partial_dcodes",
    )(ids, delta, *([dec_weight] * KS))


def grads_kernel(slots, ids, delta_ref, codes_ref, cap_ref, dpre_ref, enc_ref, dec_ref, dec_acc, enc_acc):
    j = pl.program_id(0)

    def look(s, found):
        hit = ids[s] == j
        first = jnp.logical_and(hit, found == 0)
        again = jnp.logical_and(hit, found > 0)
        tokens = pl.ds(pl.multiple_of((s // KS) * TB, TB), TB)
        mine = pl.ds(pl.multiple_of(s * TB, TB), TB)

        def tiles():
            return (
                dot(codes_ref[mine], delta_ref[tokens], 0, 0),
                dot(cap_ref[tokens], dpre_ref[mine], 0, 0),
            )

        @pl.when(first)
        def _():
            dec_acc[...], enc_acc[...] = tiles()

        @pl.when(again)
        def _():
            d, e = tiles()
            dec_acc[...] += d
            enc_acc[...] += e

        return found + hit.astype(jnp.int32)

    found = lax.fori_loop(0, slots, look, jnp.int32(0))

    @pl.when(found > 0)
    def _():
        dec_ref[...] = dec_acc[...].astype(BF16)
        enc_ref[...] = enc_acc[...].astype(BF16)

    @pl.when(found == 0)
    def _():
        dec_ref[...] = jnp.zeros(dec_ref.shape, BF16)
        enc_ref[...] = jnp.zeros(enc_ref.shape, BF16)


def gradients(ids, delta, codes, captured, dpre, lat_dev):
    features = delta.shape[1]
    slots = ids.shape[0]
    whole = pl.BlockSpec(memory_space=VMEM)
    return pl.pallas_call(
        functools.partial(grads_kernel, slots),
        grid_spec=pltpu.PrefetchScalarGridSpec(
            num_scalar_prefetch=1,
            grid=(lat_dev // LB,),
            in_specs=[whole] * 4,
            out_specs=[
                pl.BlockSpec((features, LB), lambda j, ids: (0, j)),
                pl.BlockSpec((LB, features), lambda j, ids: (j, 0)),
            ],
            scratch_shapes=[VMEM((LB, features), F32), VMEM((features, LB), F32)],
        ),
        out_shape=[
            jax.ShapeDtypeStruct((features, lat_dev), BF16),
            jax.ShapeDtypeStruct((lat_dev, features), BF16),
        ],
        compiler_params=pltpu.CompilerParams(vmem_limit_bytes=BIG),
        name="gradients",
    )(ids, delta, codes, captured, dpre)


def local(captured, enc_weight, enc_bias, dec_weight, dec_bias, block_ids, block_counts):
    n = lax.axis_size("tok")
    ids = block_ids.reshape(-1)
    counts = block_counts.reshape(-1)
    pre, bias, live = partial_pre(ids, counts, captured, enc_weight, enc_bias)
    codes = exchange(make_codes, 0, "codes_exchange", pre, bias, live)
    part = rebuild_part(ids, codes, dec_weight)
    delta = line_delta(part, captured, dec_bias, 32, 2)
    dcodes = partial_dcodes(ids, delta, dec_weight)
    dpre = exchange(make_dpre, 2, "dpre_exchange", dcodes, codes.reshape(n, -1, LB))
    return tuple(gradients(ids, delta, codes, captured, dpre, enc_weight.shape[1]))


def solution(mesh):
    in_specs = (
        P(None, "tok"),
        P("tok", "lat"),
        P("lat"),
        P("lat", "tok"),
        P("tok"),
        P(None, "lat", None),
        P(None, "lat"),
    )
    out_specs = (P("tok", "lat"), P("lat", "tok"))
    return jax.shard_map(local, mesh=mesh, in_specs=in_specs, out_specs=out_specs, check_vma=False)
```

```python
import functools

import jax
import jax.numpy as jnp
from jax import lax
from jax.experimental import pallas as pl
from jax.experimental.pallas import tpu as pltpu
from jax.sharding import PartitionSpec as P

TB = 128
LB = 128
KS = 2

SCALE_ERR = 0.0625
PENALTY = 0.05
F32 = jnp.float32
BF16 = jnp.bfloat16
MESH = pl.DeviceIdType.MESH
VMEM = pltpu.VMEM
BIG = 60 * 1024 * 1024


def dot(a, b, ca, cb):
    return lax.dot_general(a, b, (((ca,), (cb,)), ((), ())), preferred_element_type=F32)


def pre_kernel(ids, counts, cap_ref, *refs):
    enc_refs, bias_refs, dec_refs = refs[:KS], refs[KS:2 * KS], refs[2 * KS:3 * KS]
    pre_ref, bsel_ref, live_ref, pack_ref = refs[3 * KS:]
    b = pl.program_id(0)
    tiles = jnp.concatenate([r[...] for r in enc_refs], axis=1)
    pre = dot(cap_ref[...], tiles, 1, 0).astype(BF16)
    for k in range(KS):
        pre_ref[k * TB:(k + 1) * TB] = pre[:, k * LB:(k + 1) * LB]
        bsel_ref[k] = bias_refs[k][0]
        live_ref[k] = jnp.full((1, LB), (k < counts[b]).astype(F32), F32)
        pack_ref[k * LB:(k + 1) * LB] = dec_refs[k][...]


def named(k, place):
    return lambda b, ids, counts: place(ids[b * KS + k])


def partial_pre(ids, counts, captured, enc_weight, enc_bias, dec_weight):
    features = captured.shape[1]
    slots = ids.shape[0]
    step = lambda b, ids, counts: (b, 0)
    row = pl.BlockSpec((KS, 1, LB), lambda b, ids, counts: (b, 0, 0))
    return pl.pallas_call(
        pre_kernel,
        grid_spec=pltpu.PrefetchScalarGridSpec(
            num_scalar_prefetch=2,
            grid=(slots // KS,),
            in_specs=[pl.BlockSpec((TB, features), step)]
            + [pl.BlockSpec((features, LB), named(k, lambda g: (0, g))) for k in range(KS)]
            + [pl.BlockSpec((1, 1, LB), named(k, lambda g: (g, 0, 0))) for k in range(KS)]
            + [pl.BlockSpec((LB, features), named(k, lambda g: (g, 0))) for k in range(KS)],
            out_specs=[
                pl.BlockSpec((KS * TB, LB), step), row, row, pl.BlockSpec((KS * LB, features), step),
            ],
        ),
        out_shape=[
            jax.ShapeDtypeStruct((slots * TB, LB), BF16),
            jax.ShapeDtypeStruct((slots, 1, LB), F32),
            jax.ShapeDtypeStruct((slots, 1, LB), F32),
            jax.ShapeDtypeStruct((slots * LB, features), BF16),
        ],
        compiler_params=pltpu.CompilerParams(vmem_limit_bytes=BIG),
        name="partial_pre",
    )(
        ids, counts, captured, *([enc_weight] * KS), *([enc_bias.reshape(-1, 1, LB)] * KS),
        *([dec_weight] * KS),
    )


def middle_kernel(
    n, nz, chunk, lag,
    pre_ref, bias_ref, live_ref, dbias_ref, cap_hbm, dec_hbm,
    codes_ref, dpre_ref, delta_hbm,
    cap_v, dec_v, part_v, delta_v, up_in, down_in, up_out, down_out,
    pre_in, dc_out, dc_in,
    up_send, up_recv, down_send, down_recv,
    pre_send, pre_recv, code_send, code_recv, dc_send, dc_recv, dp_send, dp_recv,
    load_sem, store_sem,
):
    me = lax.axis_index("tok")
    z = lax.axis_index("lat")
    group = part_v.shape[0] // n
    per = group // chunk
    own = group // TB
    chunks = n * per
    has_low = z > 0
    has_high = z < nz - 1
    inner = jnp.logical_and(has_low, has_high)
    low = jnp.maximum(z - 1, 0)
    high = jnp.minimum(z + 1, nz - 1)

    load_dec = pltpu.make_async_copy(dec_hbm, dec_v, load_sem.at[0])
    load_cap = pltpu.make_async_copy(cap_hbm, cap_v, load_sem.at[1])
    load_dec.start()
    load_cap.start()

    barrier = pltpu.get_barrier_semaphore()
    for d in range(1, n):
        pl.semaphore_signal(barrier, inc=1, device_id={"tok": lax.rem(me + d, n)}, device_id_type=MESH)

    @pl.when(has_low)
    def _():
        pl.semaphore_signal(barrier, inc=1, device_id={"lat": low}, device_id_type=MESH)

    @pl.when(has_high)
    def _():
        pl.semaphore_signal(barrier, inc=1, device_id={"lat": high}, device_id_type=MESH)

    pl.semaphore_wait(barrier, n - 1 + has_low.astype(jnp.int32) + has_high.astype(jnp.int32))

    def tok_copy(src, dst, send, recv, d, peer):
        return pltpu.make_async_remote_copy(
            src_ref=src, dst_ref=dst, send_sem=send.at[d - 1], recv_sem=recv.at[d - 1],
            device_id={"tok": peer}, device_id_type=MESH,
        )

    outgoing = []
    for d in range(1, n):
        peer = lax.rem(me + d, n)
        copy = tok_copy(pre_ref.at[peer], pre_in.at[d - 1], pre_send, pre_recv, d, peer)
        copy.start()
        outgoing.append(copy)
    for copy in outgoing:
        copy.wait()
    total = pre_ref[me].astype(F32)
    for d in range(1, n):
        total = total + pre_in[d - 1].astype(F32)
    outs = []
    for s in range(own * KS):
        v = total[s * TB:(s + 1) * TB] + bias_ref[me * own * KS + s]
        soft = jnp.maximum(v, 0.0) + jnp.log1p(jnp.exp(-jnp.abs(v)))
        outs.append((soft * live_ref[me * own * KS + s]).astype(BF16))
    codes_ref[me] = jnp.concatenate(outs, axis=0)

    def give_codes(d):
        return tok_copy(codes_ref.at[me], codes_ref.at[me], code_send, code_recv, d, lax.rem(me + n - d, n))

    def get_codes(d, g):
        return tok_copy(codes_ref.at[g], codes_ref.at[g], code_send, code_recv, d, lax.rem(me + n - d, n))

    for d in range(1, n):
        give_codes(d).start()
    load_dec.wait()
    load_cap.wait()

    def group_of(i):
        return lax.rem(me + i, n)

    def rows(c):
        return pl.ds(pl.multiple_of(group_of(c // per) * group + lax.rem(c, per) * chunk, chunk), chunk)

    def line_copy(src, dst, send, recv, c, dev):
        return pltpu.make_async_remote_copy(
            src_ref=src.at[rows(c)], dst_ref=dst.at[rows(c)], send_sem=send.at[c], recv_sem=recv.at[c],
            device_id={"lat": dev}, device_id_type=MESH,
        )

    def up(c):
        return line_copy(up_out, up_in, up_send, up_recv, c, high)

    def up_first(c):
        return line_copy(part_v, up_in, up_send, up_recv, c, high)

    def down(c):
        return line_copy(down_out, down_in, down_send, down_recv, c, low)

    def down_first(c):
        return line_copy(part_v, down_in, down_send, down_recv, c, low)

    def block_rows(g, o, size):
        return pl.ds(pl.multiple_of((g * own + o) * size, size), size)

    def make_part(g):
        for o in range(own):
            tiles = [codes_ref[g, pl.ds((o * KS + k) * TB, TB)] for k in range(KS)]
            value = dot(jnp.concatenate(tiles, axis=1), dec_v[block_rows(g, o, KS * LB)], 1, 0)
            part_v[block_rows(g, o, TB)] = value.astype(BF16)

    def delta_copy(g):
        span = pl.ds(pl.multiple_of(g * group, group), group)
        return pltpu.make_async_copy(delta_v.at[span], delta_hbm.at[span], store_sem.at[g])

    def give_dcodes(i):
        g = group_of(i)
        return tok_copy(dc_out.at[g], dc_in.at[i - 1], dc_send, dc_recv, i, g)

    up_delay = lag * z
    down_delay = lag * (nz - 1 - z)
    first_delay = jnp.minimum(up_delay, down_delay)
    last_delay = jnp.maximum(up_delay, down_delay)

    def step(t, carry):
        cf = t - first_delay
        cu = t - up_delay
        cd = t - down_delay
        cl = t - last_delay
        stage = jnp.maximum(cf, 0) // per

        @pl.when(jnp.logical_and(jnp.logical_and(cf >= 0, cf < chunks), lax.rem(jnp.maximum(cf, 0), per) == 0))
        def _():
            @pl.when(stage > 0)
            def _():
                get_codes(stage, group_of(stage)).wait_recv()

            make_part(group_of(stage))

        @pl.when(jnp.logical_and(cu >= 0, cu < chunks))
        def _():
            @pl.when(has_low)
            def _():
                up(cu).wait_recv()

                @pl.when(has_high)
                def _():
                    up_out[rows(cu)] = (up_in[rows(cu)].astype(F32) + part_v[rows(cu)].astype(F32)).astype(BF16)
                    up(cu).start()

            @pl.when(jnp.logical_not(has_low))
            def _():
                up_first(cu).start()

        @pl.when(jnp.logical_and(cd >= 0, cd < chunks))
        def _():
            @pl.when(has_high)
            def _():
                down(cd).wait_recv()

                @pl.when(has_low)
                def _():
                    down_out[rows(cd)] = (down_in[rows(cd)].astype(F32) + part_v[rows(cd)].astype(F32)).astype(BF16)
                    down(cd).start()

            @pl.when(jnp.logical_not(has_high))
            def _():
                down_first(cd).start()

        @pl.when(jnp.logical_and(cl >= 0, cl < chunks))
        def _():
            here = part_v[rows(cl)].astype(F32) + dbias_ref[...] - cap_v[rows(cl)].astype(F32)

            @pl.when(inner)
            def _():
                both = up_in[rows(cl)].astype(F32) + down_in[rows(cl)].astype(F32)
                delta_v[rows(cl)] = (SCALE_ERR * (here + both)).astype(BF16)

            @pl.when(jnp.logical_not(has_low))
            def _():
                delta_v[rows(cl)] = (SCALE_ERR * (here + down_in[rows(cl)].astype(F32))).astype(BF16)

            @pl.when(jnp.logical_not(has_high))
            def _():
                delta_v[rows(cl)] = (SCALE_ERR * (here + up_in[rows(cl)].astype(F32))).astype(BF16)

            done = cl // per

            @pl.when(lax.rem(cl, per) == per - 1)
            def _():
                g = group_of(done)
                for o in range(own):
                    value = dot(delta_v[block_rows(g, o, TB)], dec_v[block_rows(g, o, KS * LB)], 1, 1).astype(BF16)
                    for k in range(KS):
                        dc_out[g, pl.ds((o * KS + k) * TB, TB)] = value[:, k * LB:(k + 1) * LB]

                @pl.when(done > 0)
                def _():
                    give_dcodes(done).start()

                delta_copy(g).start()

        return carry

    lax.fori_loop(0, chunks + lag * (nz - 1), step, 0)

    total = dc_out[me].astype(F32)
    for d in range(1, n):
        give_dcodes(d).wait_recv()
        total = total + dc_in[d - 1].astype(F32)
    dpre_ref[me] = ((total + PENALTY) * (1.0 - jnp.exp(-codes_ref[me].astype(F32)))).astype(BF16)

    def give_dpre(d, g):
        return tok_copy(dpre_ref.at[g], dpre_ref.at[g], dp_send, dp_recv, d, lax.rem(me + n - d, n))

    for d in range(1, n):
        give_dpre(d, me).start()

    def drain(c, carry):
        @pl.when(has_high)
        def _():
            up(c).wait_send()

        @pl.when(has_low)
        def _():
            down(c).wait_send()

        return carry

    lax.fori_loop(0, chunks, drain, 0)
    for g in range(n):
        delta_copy(g).wait()
    for d in range(1, n):
        give_codes(d).wait_send()
        give_dcodes(d).wait_send()
        give_dpre(d, me).wait_send()
        give_dpre(d, group_of(d)).wait_recv()


def middle(pre, bias, live, dec_bias, captured, pack, chunk, lag):
    n = lax.axis_size("tok")
    nz = lax.axis_size("lat")
    tokens, features = captured.shape
    rows = pre.shape[0] // n
    chunks = tokens // chunk
    whole = pl.BlockSpec(memory_space=VMEM)
    outside = pl.BlockSpec(memory_space=pltpu.HBM)
    sems = lambda count: [pltpu.SemaphoreType.DMA((count,))]
    wide = VMEM((tokens, features), BF16)
    return pl.pallas_call(
        functools.partial(middle_kernel, n, nz, chunk, lag),
        out_shape=[
            jax.ShapeDtypeStruct((n, rows, LB), BF16),
            jax.ShapeDtypeStruct((n, rows, LB), BF16),
            jax.ShapeDtypeStruct((tokens, features), BF16),
        ],
        in_specs=[whole] * 4 + [outside] * 2,
        out_specs=[whole, whole, outside],
        scratch_shapes=[wide, VMEM(pack.shape, BF16)] + [wide] * 6
        + [VMEM((n - 1, rows, LB), BF16), VMEM((n, rows, LB), BF16), VMEM((n - 1, rows, LB), BF16)]
        + sems(chunks) * 4 + sems(n - 1) * 8 + sems(2) + sems(n),
        compiler_params=pltpu.CompilerParams(
            collective_id=0, has_side_effects=True, vmem_limit_bytes=BIG
        ),
        name="middle",
    )(pre.reshape(n, rows, LB), bias, live, dec_bias.reshape(1, features), captured, pack)


def grads_kernel(slots, ids, delta_ref, codes_ref, cap_ref, dpre_ref, enc_ref, dec_ref, dec_acc, enc_acc, head, after):
    j = pl.program_id(0)

    @pl.when(j == 0)
    def _():
        def clear(g, carry):
            head[g] = -1
            return carry

        lax.fori_loop(0, pl.num_programs(0), clear, 0)
        for s in reversed(range(slots)):
            after[s] = head[ids[s]]
            head[ids[s]] = s

    def tiles(s):
        tokens = pl.ds(pl.multiple_of((s // KS) * TB, TB), TB)
        mine = pl.ds(pl.multiple_of(s * TB, TB), TB)
        return (
            dot(codes_ref[mine], delta_ref[tokens], 0, 0),
            dot(cap_ref[tokens], dpre_ref[mine], 0, 0),
        )

    start = head[j]

    @pl.when(start < 0)
    def _():
        dec_ref[...] = jnp.zeros(dec_ref.shape, BF16)
        enc_ref[...] = jnp.zeros(enc_ref.shape, BF16)

    @pl.when(start >= 0)
    def _():
        more = after[start]

        @pl.when(more < 0)
        def _():
            d, e = tiles(start)
            dec_ref[...] = d.astype(BF16)
            enc_ref[...] = e.astype(BF16)

        @pl.when(more >= 0)
        def _():
            dec_acc[...], enc_acc[...] = tiles(start)

            def add(s):
                d, e = tiles(s)
                dec_acc[...] += d
                enc_acc[...] += e
                return after[s]

            lax.while_loop(lambda s: s >= 0, add, more)
            dec_ref[...] = dec_acc[...].astype(BF16)
            enc_ref[...] = enc_acc[...].astype(BF16)


def gradients(ids, delta, codes, captured, dpre, lat_dev):
    features = delta.shape[1]
    slots = ids.shape[0]
    whole = pl.BlockSpec(memory_space=VMEM)
    return pl.pallas_call(
        functools.partial(grads_kernel, slots),
        grid_spec=pltpu.PrefetchScalarGridSpec(
            num_scalar_prefetch=1,
            grid=(lat_dev // LB,),
            in_specs=[whole] * 4,
            out_specs=[
                pl.BlockSpec((features, LB), lambda j, ids: (0, j)),
                pl.BlockSpec((LB, features), lambda j, ids: (j, 0)),
            ],
            scratch_shapes=[
                VMEM((LB, features), F32), VMEM((features, LB), F32),
                pltpu.SMEM((lat_dev // LB,), jnp.int32), pltpu.SMEM((slots,), jnp.int32),
            ],
        ),
        out_shape=[
            jax.ShapeDtypeStruct((features, lat_dev), BF16),
            jax.ShapeDtypeStruct((lat_dev, features), BF16),
        ],
        compiler_params=pltpu.CompilerParams(vmem_limit_bytes=BIG),
        name="gradients",
    )(ids, delta, codes, captured, dpre)


def local(captured, enc_weight, enc_bias, dec_weight, dec_bias, block_ids, block_counts):
    ids = block_ids.reshape(-1)
    counts = block_counts.reshape(-1)
    pre, bias, live, pack = partial_pre(ids, counts, captured, enc_weight, enc_bias, dec_weight)
    codes, dpre, delta = middle(pre, bias, live, dec_bias, captured, pack, 16, 4)
    codes, dpre = codes.reshape(-1, LB), dpre.reshape(-1, LB)
    return tuple(gradients(ids, delta, codes, captured, dpre, enc_weight.shape[1]))


def solution(mesh):
    in_specs = (
        P(None, "tok"),
        P("tok", "lat"),
        P("lat"),
        P("lat", "tok"),
        P("tok"),
        P(None, "lat", None),
        P(None, "lat"),
    )
    out_specs = (P("tok", "lat"), P("lat", "tok"))
    return jax.shard_map(local, mesh=mesh, in_specs=in_specs, out_specs=out_specs, check_vma=False)
```

```python
import functools

import jax
import jax.numpy as jnp
from jax import lax
from jax.experimental import pallas as pl
from jax.experimental.pallas import tpu as pltpu
from jax.sharding import PartitionSpec as P

TB = 128
LB = 128
KS = 2

SCALE_ERR = 0.0625
PENALTY = 0.05
F32 = jnp.float32
BF16 = jnp.bfloat16
MESH = pl.DeviceIdType.MESH
VMEM = pltpu.VMEM
BIG = 60 * 1024 * 1024


def dot(a, b, ca, cb):
    return lax.dot_general(a, b, (((ca,), (cb,)), ((), ())), preferred_element_type=F32)


def pre_kernel(ids, counts, cap_ref, *refs):
    enc_refs, bias_refs = refs[:KS], refs[KS:2 * KS]
    pre_ref, bsel_ref, live_ref, order_ref, tile_ref, first_ref, place = refs[2 * KS:]
    b = pl.program_id(0)

    @pl.when(b == 0)
    def _():
        def clear(g, carry):
            place[g] = 0
            return carry

        def count(s, carry):
            place[ids[s]] += 1
            return carry

        def unnamed(g, at):
            @pl.when(place[g] == 0)
            def _():
                tile_ref[at] = g

            return at + (place[g] == 0).astype(jnp.int32)

        def taken(g, at):
            @pl.when(place[g] > 0)
            def _():
                tile_ref[at] = g

            return at + (place[g] > 0).astype(jnp.int32)

        def offset(g, seen):
            here = place[g]
            place[g] = seen
            first_ref[g] = seen
            return seen + here

        def put(s, carry):
            at = place[ids[s]]
            order_ref[at] = s
            place[ids[s]] = at + 1
            return carry

        slots, groups = order_ref.shape[0], place.shape[0]
        lax.fori_loop(0, groups, clear, 0)
        lax.fori_loop(0, slots, count, 0)
        lax.fori_loop(0, groups, taken, lax.fori_loop(0, groups, unnamed, jnp.int32(0)))
        first_ref[groups] = lax.fori_loop(0, groups, offset, jnp.int32(0))
        lax.fori_loop(0, slots, put, 0)

    tiles = jnp.concatenate([r[...] for r in enc_refs], axis=1)
    pre = dot(cap_ref[...], tiles, 1, 0).astype(BF16)
    for k in range(KS):
        pre_ref[k * TB:(k + 1) * TB] = pre[:, k * LB:(k + 1) * LB]
        bsel_ref[k] = bias_refs[k][0]
        live_ref[k] = jnp.full((1, LB), (k < counts[b]).astype(F32), F32)


def named(k, place):
    return lambda b, ids, counts: place(ids[b * KS + k])


def partial_pre(ids, counts, captured, enc_weight, enc_bias):
    features = captured.shape[1]
    slots = ids.shape[0]
    groups = enc_weight.shape[1] // LB
    step = lambda b, ids, counts: (b, 0)
    row = pl.BlockSpec((KS, 1, LB), lambda b, ids, counts: (b, 0, 0))
    return pl.pallas_call(
        pre_kernel,
        grid_spec=pltpu.PrefetchScalarGridSpec(
            num_scalar_prefetch=2,
            grid=(slots // KS,),
            in_specs=[pl.BlockSpec((TB, features), step)]
            + [pl.BlockSpec((features, LB), named(k, lambda g: (0, g))) for k in range(KS)]
            + [pl.BlockSpec((1, 1, LB), named(k, lambda g: (g, 0, 0))) for k in range(KS)],
            out_specs=[
                pl.BlockSpec((KS * TB, LB), step), row, row,
            ] + [pl.BlockSpec(memory_space=pltpu.SMEM)] * 3,
            scratch_shapes=[pltpu.SMEM((groups,), jnp.int32)],
        ),
        out_shape=[
            jax.ShapeDtypeStruct((slots * TB, LB), BF16),
            jax.ShapeDtypeStruct((slots, 1, LB), F32),
            jax.ShapeDtypeStruct((slots, 1, LB), F32),
            jax.ShapeDtypeStruct((slots,), jnp.int32),
            jax.ShapeDtypeStruct((groups,), jnp.int32),
            jax.ShapeDtypeStruct((groups + 1,), jnp.int32),
        ],
        compiler_params=pltpu.CompilerParams(vmem_limit_bytes=BIG),
        name="partial_pre",
    )(
        ids, counts, captured, *([enc_weight] * KS), *([enc_bias.reshape(-1, 1, LB)] * KS),
    )


def middle_kernel(
    n, nz, chunk, lag,
    ids, pre_ref, bias_ref, live_ref, dbias_ref, cap_hbm, dec_hbm,
    codes_ref, dpre_ref, delta_hbm,
    cap_v, dec_v, part_v, delta_v, up_in, down_in, up_out, down_out,
    pre_in, dc_out, dc_in,
    up_send, up_recv, down_send, down_recv,
    pre_send, pre_recv, code_send, code_recv, dc_send, dc_recv, dp_send, dp_recv,
    load_sem, store_sem,
):
    me = lax.axis_index("tok")
    z = lax.axis_index("lat")
    group = part_v.shape[0] // n
    per = group // chunk
    own = group // TB
    chunks = n * per
    has_low = z > 0
    has_high = z < nz - 1
    inner = jnp.logical_and(has_low, has_high)
    low = jnp.maximum(z - 1, 0)
    high = jnp.minimum(z + 1, nz - 1)

    load_dec = pltpu.make_async_copy(dec_hbm, dec_v, load_sem.at[0])
    load_cap = pltpu.make_async_copy(cap_hbm, cap_v, load_sem.at[1])
    load_dec.start()
    load_cap.start()

    barrier = pltpu.get_barrier_semaphore()
    for d in range(1, n):
        pl.semaphore_signal(barrier, inc=1, device_id={"tok": lax.rem(me + d, n)}, device_id_type=MESH)

    @pl.when(has_low)
    def _():
        pl.semaphore_signal(barrier, inc=1, device_id={"lat": low}, device_id_type=MESH)

    @pl.when(has_high)
    def _():
        pl.semaphore_signal(barrier, inc=1, device_id={"lat": high}, device_id_type=MESH)

    pl.semaphore_wait(barrier, n - 1 + has_low.astype(jnp.int32) + has_high.astype(jnp.int32))

    def tok_copy(src, dst, send, recv, d, peer):
        return pltpu.make_async_remote_copy(
            src_ref=src, dst_ref=dst, send_sem=send.at[d - 1], recv_sem=recv.at[d - 1],
            device_id={"tok": peer}, device_id_type=MESH,
        )

    outgoing = []
    for d in range(1, n):
        peer = lax.rem(me + d, n)
        copy = tok_copy(pre_ref.at[peer], pre_in.at[d - 1], pre_send, pre_recv, d, peer)
        copy.start()
        outgoing.append(copy)
    for copy in outgoing:
        copy.wait()
    total = pre_ref[me].astype(F32)
    for d in range(1, n):
        total = total + pre_in[d - 1].astype(F32)
    outs = []
    for s in range(own * KS):
        v = total[s * TB:(s + 1) * TB] + bias_ref[me * own * KS + s]
        soft = jnp.maximum(v, 0.0) + jnp.log1p(jnp.exp(-jnp.abs(v)))
        outs.append((soft * live_ref[me * own * KS + s]).astype(BF16))
    codes_ref[me] = jnp.concatenate(outs, axis=0)

    def give_codes(d):
        return tok_copy(codes_ref.at[me], codes_ref.at[me], code_send, code_recv, d, lax.rem(me + n - d, n))

    def get_codes(d, g):
        return tok_copy(codes_ref.at[g], codes_ref.at[g], code_send, code_recv, d, lax.rem(me + n - d, n))

    for d in range(1, n):
        give_codes(d).start()
    load_dec.wait()
    load_cap.wait()

    def group_of(i):
        return lax.rem(me + i, n)

    def rows(c):
        return pl.ds(pl.multiple_of(group_of(c // per) * group + lax.rem(c, per) * chunk, chunk), chunk)

    def line_copy(src, dst, send, recv, c, dev):
        return pltpu.make_async_remote_copy(
            src_ref=src.at[rows(c)], dst_ref=dst.at[rows(c)], send_sem=send.at[c], recv_sem=recv.at[c],
            device_id={"lat": dev}, device_id_type=MESH,
        )

    def up(c):
        return line_copy(up_out, up_in, up_send, up_recv, c, high)

    def up_first(c):
        return line_copy(part_v, up_in, up_send, up_recv, c, high)

    def down(c):
        return line_copy(down_out, down_in, down_send, down_recv, c, low)

    def down_first(c):
        return line_copy(part_v, down_in, down_send, down_recv, c, low)

    def block_rows(g, o, size):
        return pl.ds(pl.multiple_of((g * own + o) * size, size), size)

    def dec_tile(g, o):
        first = (g * own + o) * KS
        return jnp.concatenate([dec_v[ids[first + k]] for k in range(KS)], axis=0)

    def make_part(g):
        for o in range(own):
            tiles = [codes_ref[g, pl.ds((o * KS + k) * TB, TB)] for k in range(KS)]
            value = dot(jnp.concatenate(tiles, axis=1), dec_tile(g, o), 1, 0)
            part_v[block_rows(g, o, TB)] = value.astype(BF16)

    def delta_copy(g):
        span = pl.ds(pl.multiple_of(g * group, group), group)
        return pltpu.make_async_copy(delta_v.at[span], delta_hbm.at[span], store_sem.at[g])

    def give_dcodes(i):
        g = group_of(i)
        return tok_copy(dc_out.at[g], dc_in.at[i - 1], dc_send, dc_recv, i, g)

    up_delay = lag * z
    down_delay = lag * (nz - 1 - z)
    first_delay = jnp.minimum(up_delay, down_delay)
    last_delay = jnp.maximum(up_delay, down_delay)

    def step(t, carry):
        cf = t - first_delay
        cu = t - up_delay
        cd = t - down_delay
        cl = t - last_delay
        stage = jnp.maximum(cf, 0) // per

        @pl.when(jnp.logical_and(jnp.logical_and(cf >= 0, cf < chunks), lax.rem(jnp.maximum(cf, 0), per) == 0))
        def _():
            @pl.when(stage > 0)
            def _():
                get_codes(stage, group_of(stage)).wait_recv()

            make_part(group_of(stage))

        @pl.when(jnp.logical_and(cu >= 0, cu < chunks))
        def _():
            @pl.when(has_low)
            def _():
                up(cu).wait_recv()

                @pl.when(has_high)
                def _():
                    up_out[rows(cu)] = (up_in[rows(cu)].astype(F32) + part_v[rows(cu)].astype(F32)).astype(BF16)
                    up(cu).start()

            @pl.when(jnp.logical_not(has_low))
            def _():
                up_first(cu).start()

        @pl.when(jnp.logical_and(cd >= 0, cd < chunks))
        def _():
            @pl.when(has_high)
            def _():
                down(cd).wait_recv()

                @pl.when(has_low)
                def _():
                    down_out[rows(cd)] = (down_in[rows(cd)].astype(F32) + part_v[rows(cd)].astype(F32)).astype(BF16)
                    down(cd).start()

            @pl.when(jnp.logical_not(has_high))
            def _():
                down_first(cd).start()

        @pl.when(jnp.logical_and(cl >= 0, cl < chunks))
        def _():
            here = part_v[rows(cl)].astype(F32) + dbias_ref[...] - cap_v[rows(cl)].astype(F32)

            @pl.when(inner)
            def _():
                both = up_in[rows(cl)].astype(F32) + down_in[rows(cl)].astype(F32)
                delta_v[rows(cl)] = (SCALE_ERR * (here + both)).astype(BF16)

            @pl.when(jnp.logical_not(has_low))
            def _():
                delta_v[rows(cl)] = (SCALE_ERR * (here + down_in[rows(cl)].astype(F32))).astype(BF16)

            @pl.when(jnp.logical_not(has_high))
            def _():
                delta_v[rows(cl)] = (SCALE_ERR * (here + up_in[rows(cl)].astype(F32))).astype(BF16)

            done = cl // per

            @pl.when(lax.rem(cl, per) == per - 1)
            def _():
                g = group_of(done)
                for o in range(own):
                    value = dot(delta_v[block_rows(g, o, TB)], dec_tile(g, o), 1, 1).astype(BF16)
                    for k in range(KS):
                        dc_out[g, pl.ds((o * KS + k) * TB, TB)] = value[:, k * LB:(k + 1) * LB]

                @pl.when(done > 0)
                def _():
                    give_dcodes(done).start()

                delta_copy(g).start()

        return carry

    lax.fori_loop(0, chunks + lag * (nz - 1), step, 0)

    total = dc_out[me].astype(F32)
    for d in range(1, n):
        give_dcodes(d).wait_recv()
        total = total + dc_in[d - 1].astype(F32)
    dpre_ref[me] = ((total + PENALTY) * (1.0 - jnp.exp(-codes_ref[me].astype(F32)))).astype(BF16)

    def give_dpre(d, g):
        return tok_copy(dpre_ref.at[g], dpre_ref.at[g], dp_send, dp_recv, d, lax.rem(me + n - d, n))

    for d in range(1, n):
        give_dpre(d, me).start()

    def drain(c, carry):
        @pl.when(has_high)
        def _():
            up(c).wait_send()

        @pl.when(has_low)
        def _():
            down(c).wait_send()

        return carry

    lax.fori_loop(0, chunks, drain, 0)
    for g in range(n):
        delta_copy(g).wait()
    for d in range(1, n):
        give_codes(d).wait_send()
        give_dcodes(d).wait_send()
        give_dpre(d, me).wait_send()
        give_dpre(d, group_of(d)).wait_recv()


def middle(ids, pre, bias, live, dec_bias, captured, dec_weight, chunk, lag):
    n = lax.axis_size("tok")
    nz = lax.axis_size("lat")
    tokens, features = captured.shape
    rows = pre.shape[0] // n
    lat_dev = dec_weight.shape[0]
    chunks = tokens // chunk
    whole = pl.BlockSpec(memory_space=VMEM)
    outside = pl.BlockSpec(memory_space=pltpu.HBM)
    sems = lambda count: [pltpu.SemaphoreType.DMA((count,))]
    wide = VMEM((tokens, features), BF16)
    return pl.pallas_call(
        functools.partial(middle_kernel, n, nz, chunk, lag),
        out_shape=[
            jax.ShapeDtypeStruct((n, rows, LB), BF16),
            jax.ShapeDtypeStruct((n, rows, LB), BF16),
            jax.ShapeDtypeStruct((tokens, features), BF16),
        ],
        in_specs=[pl.BlockSpec(memory_space=pltpu.SMEM)] + [whole] * 4 + [outside] * 2,
        out_specs=[whole, whole, outside],
        scratch_shapes=[wide, VMEM((lat_dev // LB, LB, features), BF16)] + [wide] * 6
        + [VMEM((n - 1, rows, LB), BF16), VMEM((n, rows, LB), BF16), VMEM((n - 1, rows, LB), BF16)]
        + sems(chunks) * 4 + sems(n - 1) * 8 + sems(2) + sems(n),
        compiler_params=pltpu.CompilerParams(
            collective_id=0, has_side_effects=True, vmem_limit_bytes=BIG
        ),
        name="middle",
    )(
        ids, pre.reshape(n, rows, LB), bias, live, dec_bias.reshape(1, features), captured,
        dec_weight.reshape(-1, LB, features),
    )


def grads_kernel(
    order, tile, first, delta_hbm, codes_ref, cap_hbm, dpre_ref,
    enc_ref, dec_ref, delta_v, cap_v, dec_acc, enc_acc, state, delta_sem, cap_sem,
):
    i = pl.program_id(0)
    start = first[tile[i]]
    stop = first[tile[i] + 1]

    def loads(b):
        span = pl.ds(pl.multiple_of(b * TB, TB), TB)
        return (
            pltpu.make_async_copy(delta_hbm.at[span], delta_v.at[span], delta_sem.at[b]),
            pltpu.make_async_copy(cap_hbm.at[span], cap_v.at[span], cap_sem.at[b]),
        )

    @pl.when(i == 0)
    def _():
        def clear(b, carry):
            state[b] = 0
            return carry

        def begin(t, carry):
            b = order[t] // KS

            @pl.when(state[b] == 0)
            def _():
                for copy in loads(b):
                    copy.start()
                state[b] = 1

            return carry

        lax.fori_loop(0, state.shape[0], clear, 0)
        lax.fori_loop(0, order.shape[0], begin, 0)

    def tiles(t):
        s = order[t]
        b = s // KS

        @pl.when(state[b] == 1)
        def _():
            for copy in loads(b):
                copy.wait()
            state[b] = 2

        tokens = pl.ds(pl.multiple_of(b * TB, TB), TB)
        mine = pl.ds(pl.multiple_of(s * TB, TB), TB)
        return (
            dot(codes_ref[mine], delta_v[tokens], 0, 0),
            dot(cap_v[tokens], dpre_ref[mine], 0, 0),
        )

    @pl.when(stop == start)
    def _():
        dec_ref[...] = jnp.zeros(dec_ref.shape, BF16)
        enc_ref[...] = jnp.zeros(enc_ref.shape, BF16)

    @pl.when(stop == start + 1)
    def _():
        d, e = tiles(start)
        dec_ref[...] = d.astype(BF16)
        enc_ref[...] = e.astype(BF16)

    @pl.when(stop > start + 1)
    def _():
        dec_acc[...], enc_acc[...] = tiles(start)

        def add(t, carry):
            d, e = tiles(t)
            dec_acc[...] += d
            enc_acc[...] += e
            return carry

        lax.fori_loop(start + 1, stop, add, 0)
        dec_ref[...] = dec_acc[...].astype(BF16)
        enc_ref[...] = enc_acc[...].astype(BF16)


def gradients(order, tile, first, delta, codes, captured, dpre):
    tokens, features = delta.shape
    blocks = tokens // TB
    groups = tile.shape[0]
    whole = pl.BlockSpec(memory_space=VMEM)
    outside = pl.BlockSpec(memory_space=pltpu.HBM)
    return pl.pallas_call(
        grads_kernel,
        grid_spec=pltpu.PrefetchScalarGridSpec(
            num_scalar_prefetch=3,
            grid=(groups,),
            in_specs=[outside, whole, outside, whole],
            out_specs=[
                pl.BlockSpec((features, LB), lambda i, order, tile, first: (0, tile[i])),
                pl.BlockSpec((LB, features), lambda i, order, tile, first: (tile[i], 0)),
            ],
            scratch_shapes=[
                VMEM((tokens, features), BF16), VMEM((tokens, features), BF16),
                VMEM((LB, features), F32), VMEM((features, LB), F32),
                pltpu.SMEM((blocks,), jnp.int32),
                pltpu.SemaphoreType.DMA((blocks,)), pltpu.SemaphoreType.DMA((blocks,)),
            ],
        ),
        out_shape=[
            jax.ShapeDtypeStruct((features, groups * LB), BF16),
            jax.ShapeDtypeStruct((groups * LB, features), BF16),
        ],
        compiler_params=pltpu.CompilerParams(vmem_limit_bytes=BIG),
        name="gradients",
    )(order, tile, first, delta, codes, captured, dpre)


def local(captured, enc_weight, enc_bias, dec_weight, dec_bias, block_ids, block_counts):
    ids = block_ids.reshape(-1)
    counts = block_counts.reshape(-1)
    pre, bias, live, order, tile, first = partial_pre(ids, counts, captured, enc_weight, enc_bias)
    codes, dpre, delta = middle(ids, pre, bias, live, dec_bias, captured, dec_weight, 16, 4)
    codes, dpre = codes.reshape(-1, LB), dpre.reshape(-1, LB)
    return tuple(gradients(order, tile, first, delta, codes, captured, dpre))


def solution(mesh):
    in_specs = (
        P(None, "tok"),
        P("tok", "lat"),
        P("lat"),
        P("lat", "tok"),
        P("tok"),
        P(None, "lat", None),
        P(None, "lat"),
    )
    out_specs = (P("tok", "lat"), P("lat", "tok"))
    return jax.shard_map(local, mesh=mesh, in_specs=in_specs, out_specs=out_specs, check_vma=False)
```

```python
import functools

import jax
import jax.numpy as jnp
from jax import lax
from jax.experimental import pallas as pl
from jax.experimental.pallas import tpu as pltpu
from jax.sharding import PartitionSpec as P

TB = 128
LB = 128
KS = 2

SCALE_ERR = 0.0625
PENALTY = 0.05
F32 = jnp.float32
BF16 = jnp.bfloat16
MESH = pl.DeviceIdType.MESH
VMEM = pltpu.VMEM
BIG = 60 * 1024 * 1024


def dot(a, b, ca, cb):
    return lax.dot_general(a, b, (((ca,), (cb,)), ((), ())), preferred_element_type=F32)


def pre_kernel(ids, counts, cap_ref, *refs):
    enc_refs, bias_refs = refs[:KS], refs[KS:2 * KS]
    pre_ref, bsel_ref, live_ref, order_ref, tile_ref, first_ref, place = refs[2 * KS:]
    b = pl.program_id(0)

    @pl.when(b == 0)
    def _():
        def clear(g, carry):
            place[g] = 0
            return carry

        def count(s, carry):
            place[ids[s]] += 1
            return carry

        def free(g, seen):
            return seen + (place[g] == 0).astype(jnp.int32)

        def visit(g, seen):
            named_one = place[g] > 0
            taken = g - seen
            late = jnp.where(taken < pairs, lead + 2 * taken + 1, unnamed + taken)
            early = jnp.where(seen < lead, seen, 2 * seen - lead)
            tile_ref[jnp.where(named_one, late, early)] = g
            return seen + 1 - named_one.astype(jnp.int32)

        def offset(g, seen):
            here = place[g]
            place[g] = seen
            first_ref[g] = seen
            return seen + here

        def put(s, carry):
            at = place[ids[s]]
            order_ref[at] = s
            place[ids[s]] = at + 1
            return carry

        slots, groups = order_ref.shape[0], place.shape[0]
        lax.fori_loop(0, groups, clear, 0)
        lax.fori_loop(0, slots, count, 0)
        unnamed = lax.fori_loop(0, groups, free, jnp.int32(0))
        lead = jnp.maximum(2 * unnamed - groups, 0)
        pairs = unnamed - lead
        lax.fori_loop(0, groups, visit, jnp.int32(0))
        first_ref[groups] = lax.fori_loop(0, groups, offset, jnp.int32(0))
        lax.fori_loop(0, slots, put, 0)

    tiles = jnp.concatenate([r[...] for r in enc_refs], axis=1)
    pre = dot(cap_ref[...], tiles, 1, 0).astype(BF16)
    for k in range(KS):
        pre_ref[k * TB:(k + 1) * TB] = pre[:, k * LB:(k + 1) * LB]
        bsel_ref[k] = bias_refs[k][0]
        live_ref[k] = jnp.full((1, LB), (k < counts[b]).astype(F32), F32)


def named(k, place):
    return lambda b, ids, counts: place(ids[b * KS + k])


def partial_pre(ids, counts, captured, enc_weight, enc_bias):
    features = captured.shape[1]
    slots = ids.shape[0]
    groups = enc_weight.shape[1] // LB
    step = lambda b, ids, counts: (b, 0)
    row = pl.BlockSpec((KS, 1, LB), lambda b, ids, counts: (b, 0, 0))
    return pl.pallas_call(
        pre_kernel,
        grid_spec=pltpu.PrefetchScalarGridSpec(
            num_scalar_prefetch=2,
            grid=(slots // KS,),
            in_specs=[pl.BlockSpec((TB, features), step)]
            + [pl.BlockSpec((features, LB), named(k, lambda g: (0, g))) for k in range(KS)]
            + [pl.BlockSpec((1, 1, LB), named(k, lambda g: (g, 0, 0))) for k in range(KS)],
            out_specs=[
                pl.BlockSpec((KS * TB, LB), step), row, row,
            ] + [pl.BlockSpec(memory_space=pltpu.SMEM)] * 3,
            scratch_shapes=[pltpu.SMEM((groups,), jnp.int32)],
        ),
        out_shape=[
            jax.ShapeDtypeStruct((slots * TB, LB), BF16),
            jax.ShapeDtypeStruct((slots, 1, LB), F32),
            jax.ShapeDtypeStruct((slots, 1, LB), F32),
            jax.ShapeDtypeStruct((slots,), jnp.int32),
            jax.ShapeDtypeStruct((groups,), jnp.int32),
            jax.ShapeDtypeStruct((groups + 1,), jnp.int32),
        ],
        compiler_params=pltpu.CompilerParams(vmem_limit_bytes=BIG),
        name="partial_pre",
    )(
        ids, counts, captured, *([enc_weight] * KS), *([enc_bias.reshape(-1, 1, LB)] * KS),
    )


def middle_kernel(
    n, nz, chunk, lag,
    ids, pre_ref, bias_ref, live_ref, dbias_ref, cap_hbm, dec_hbm,
    codes_ref, dpre_ref, delta_hbm,
    cap_v, dec_v, part_v, delta_v, up_in, down_in, up_out, down_out,
    pre_in, dc_out, dc_in,
    up_send, up_recv, down_send, down_recv,
    pre_send, pre_recv, code_send, code_recv, dc_send, dc_recv, dp_send, dp_recv,
    load_sem, store_sem,
):
    me = lax.axis_index("tok")
    z = lax.axis_index("lat")
    group = part_v.shape[0] // n
    per = group // chunk
    own = group // TB
    chunks = n * per
    has_low = z > 0
    has_high = z < nz - 1
    inner = jnp.logical_and(has_low, has_high)
    low = jnp.maximum(z - 1, 0)
    high = jnp.minimum(z + 1, nz - 1)

    load_dec = pltpu.make_async_copy(dec_hbm, dec_v, load_sem.at[0])
    load_cap = pltpu.make_async_copy(cap_hbm, cap_v, load_sem.at[1])
    load_dec.start()
    load_cap.start()

    barrier = pltpu.get_barrier_semaphore()
    for d in range(1, n):
        pl.semaphore_signal(barrier, inc=1, device_id={"tok": lax.rem(me + d, n)}, device_id_type=MESH)

    @pl.when(has_low)
    def _():
        pl.semaphore_signal(barrier, inc=1, device_id={"lat": low}, device_id_type=MESH)

    @pl.when(has_high)
    def _():
        pl.semaphore_signal(barrier, inc=1, device_id={"lat": high}, device_id_type=MESH)

    pl.semaphore_wait(barrier, n - 1 + has_low.astype(jnp.int32) + has_high.astype(jnp.int32))

    def tok_copy(src, dst, send, recv, d, peer):
        return pltpu.make_async_remote_copy(
            src_ref=src, dst_ref=dst, send_sem=send.at[d - 1], recv_sem=recv.at[d - 1],
            device_id={"tok": peer}, device_id_type=MESH,
        )

    outgoing = []
    for d in range(1, n):
        peer = lax.rem(me + d, n)
        copy = tok_copy(pre_ref.at[peer], pre_in.at[d - 1], pre_send, pre_recv, d, peer)
        copy.start()
        outgoing.append(copy)
    for copy in outgoing:
        copy.wait()
    total = pre_ref[me].astype(F32)
    for d in range(1, n):
        total = total + pre_in[d - 1].astype(F32)
    outs = []
    for s in range(own * KS):
        v = total[s * TB:(s + 1) * TB] + bias_ref[me * own * KS + s]
        soft = jnp.maximum(v, 0.0) + jnp.log1p(jnp.exp(-jnp.abs(v)))
        outs.append((soft * live_ref[me * own * KS + s]).astype(BF16))
    codes_ref[me] = jnp.concatenate(outs, axis=0)

    def give_codes(d):
        return tok_copy(codes_ref.at[me], codes_ref.at[me], code_send, code_recv, d, lax.rem(me + n - d, n))

    def get_codes(d, g):
        return tok_copy(codes_ref.at[g], codes_ref.at[g], code_send, code_recv, d, lax.rem(me + n - d, n))

    for d in range(1, n):
        give_codes(d).start()
    load_dec.wait()
    load_cap.wait()

    def group_of(i):
        return lax.rem(me + i, n)

    def rows(c):
        return pl.ds(pl.multiple_of(group_of(c // per) * group + lax.rem(c, per) * chunk, chunk), chunk)

    def line_copy(src, dst, send, recv, c, dev):
        return pltpu.make_async_remote_copy(
            src_ref=src.at[rows(c)], dst_ref=dst.at[rows(c)], send_sem=send.at[c], recv_sem=recv.at[c],
            device_id={"lat": dev}, device_id_type=MESH,
        )

    def up(c):
        return line_copy(up_out, up_in, up_send, up_recv, c, high)

    def up_first(c):
        return line_copy(part_v, up_in, up_send, up_recv, c, high)

    def down(c):
        return line_copy(down_out, down_in, down_send, down_recv, c, low)

    def down_first(c):
        return line_copy(part_v, down_in, down_send, down_recv, c, low)

    def block_rows(g, o, size):
        return pl.ds(pl.multiple_of((g * own + o) * size, size), size)

    def dec_tile(g, o):
        first = (g * own + o) * KS
        return jnp.concatenate([dec_v[ids[first + k]] for k in range(KS)], axis=0)

    def make_part(g):
        for o in range(own):
            tiles = [codes_ref[g, pl.ds((o * KS + k) * TB, TB)] for k in range(KS)]
            value = dot(jnp.concatenate(tiles, axis=1), dec_tile(g, o), 1, 0)
            part_v[block_rows(g, o, TB)] = value.astype(BF16)

    def delta_copy(g):
        span = pl.ds(pl.multiple_of(g * group, group), group)
        return pltpu.make_async_copy(delta_v.at[span], delta_hbm.at[span], store_sem.at[g])

    def give_dcodes(i):
        g = group_of(i)
        return tok_copy(dc_out.at[g], dc_in.at[i - 1], dc_send, dc_recv, i, g)

    up_delay = lag * z
    down_delay = lag * (nz - 1 - z)
    first_delay = jnp.minimum(up_delay, down_delay)
    last_delay = jnp.maximum(up_delay, down_delay)

    def step(t, carry):
        cf = t - first_delay
        cu = t - up_delay
        cd = t - down_delay
        cl = t - last_delay
        stage = jnp.maximum(cf, 0) // per

        @pl.when(jnp.logical_and(jnp.logical_and(cf >= 0, cf < chunks), lax.rem(jnp.maximum(cf, 0), per) == 0))
        def _():
            @pl.when(stage > 0)
            def _():
                get_codes(stage, group_of(stage)).wait_recv()

            make_part(group_of(stage))

        @pl.when(jnp.logical_and(cu >= 0, cu < chunks))
        def _():
            @pl.when(has_low)
            def _():
                up(cu).wait_recv()

                @pl.when(has_high)
                def _():
                    up_out[rows(cu)] = (up_in[rows(cu)].astype(F32) + part_v[rows(cu)].astype(F32)).astype(BF16)
                    up(cu).start()

            @pl.when(jnp.logical_not(has_low))
            def _():
                up_first(cu).start()

        @pl.when(jnp.logical_and(cd >= 0, cd < chunks))
        def _():
            @pl.when(has_high)
            def _():
                down(cd).wait_recv()

                @pl.when(has_low)
                def _():
                    down_out[rows(cd)] = (down_in[rows(cd)].astype(F32) + part_v[rows(cd)].astype(F32)).astype(BF16)
                    down(cd).start()

            @pl.when(jnp.logical_not(has_high))
            def _():
                down_first(cd).start()

        @pl.when(jnp.logical_and(cl >= 0, cl < chunks))
        def _():
            here = part_v[rows(cl)].astype(F32) + dbias_ref[...] - cap_v[rows(cl)].astype(F32)

            @pl.when(inner)
            def _():
                both = up_in[rows(cl)].astype(F32) + down_in[rows(cl)].astype(F32)
                delta_v[rows(cl)] = (SCALE_ERR * (here + both)).astype(BF16)

            @pl.when(jnp.logical_not(has_low))
            def _():
                delta_v[rows(cl)] = (SCALE_ERR * (here + down_in[rows(cl)].astype(F32))).astype(BF16)

            @pl.when(jnp.logical_not(has_high))
            def _():
                delta_v[rows(cl)] = (SCALE_ERR * (here + up_in[rows(cl)].astype(F32))).astype(BF16)

            done = cl // per

            @pl.when(lax.rem(cl, per) == per - 1)
            def _():
                g = group_of(done)
                for o in range(own):
                    value = dot(delta_v[block_rows(g, o, TB)], dec_tile(g, o), 1, 1).astype(BF16)
                    for k in range(KS):
                        dc_out[g, pl.ds((o * KS + k) * TB, TB)] = value[:, k * LB:(k + 1) * LB]

                @pl.when(done > 0)
                def _():
                    give_dcodes(done).start()

                delta_copy(g).start()

        return carry

    lax.fori_loop(0, chunks + lag * (nz - 1), step, 0)

    total = dc_out[me].astype(F32)
    for d in range(1, n):
        give_dcodes(d).wait_recv()
        total = total + dc_in[d - 1].astype(F32)
    dpre_ref[me] = ((total + PENALTY) * (1.0 - jnp.exp(-codes_ref[me].astype(F32)))).astype(BF16)

    def give_dpre(d, g):
        return tok_copy(dpre_ref.at[g], dpre_ref.at[g], dp_send, dp_recv, d, lax.rem(me + n - d, n))

    for d in range(1, n):
        give_dpre(d, me).start()

    def drain(c, carry):
        @pl.when(has_high)
        def _():
            up(c).wait_send()

        @pl.when(has_low)
        def _():
            down(c).wait_send()

        return carry

    lax.fori_loop(0, chunks, drain, 0)
    for g in range(n):
        delta_copy(g).wait()
    for d in range(1, n):
        give_codes(d).wait_send()
        give_dcodes(d).wait_send()
        give_dpre(d, me).wait_send()
        give_dpre(d, group_of(d)).wait_recv()


def middle(ids, pre, bias, live, dec_bias, captured, dec_weight, chunk, lag):
    n = lax.axis_size("tok")
    nz = lax.axis_size("lat")
    tokens, features = captured.shape
    rows = pre.shape[0] // n
    lat_dev = dec_weight.shape[0]
    chunks = tokens // chunk
    whole = pl.BlockSpec(memory_space=VMEM)
    outside = pl.BlockSpec(memory_space=pltpu.HBM)
    sems = lambda count: [pltpu.SemaphoreType.DMA((count,))]
    wide = VMEM((tokens, features), BF16)
    return pl.pallas_call(
        functools.partial(middle_kernel, n, nz, chunk, lag),
        out_shape=[
            jax.ShapeDtypeStruct((n, rows, LB), BF16),
            jax.ShapeDtypeStruct((n, rows, LB), BF16),
            jax.ShapeDtypeStruct((tokens, features), BF16),
        ],
        in_specs=[pl.BlockSpec(memory_space=pltpu.SMEM)] + [whole] * 4 + [outside] * 2,
        out_specs=[whole, whole, outside],
        scratch_shapes=[wide, VMEM((lat_dev // LB, LB, features), BF16)] + [wide] * 6
        + [VMEM((n - 1, rows, LB), BF16), VMEM((n, rows, LB), BF16), VMEM((n - 1, rows, LB), BF16)]
        + sems(chunks) * 4 + sems(n - 1) * 8 + sems(2) + sems(n),
        compiler_params=pltpu.CompilerParams(
            collective_id=0, has_side_effects=True, vmem_limit_bytes=BIG
        ),
        name="middle",
    )(
        ids, pre.reshape(n, rows, LB), bias, live, dec_bias.reshape(1, features), captured,
        dec_weight.reshape(-1, LB, features),
    )


def grads_kernel(
    order, tile, first, delta_hbm, codes_ref, cap_hbm, dpre_ref,
    enc_ref, dec_ref, delta_v, cap_v, dec_acc, enc_acc, state, delta_sem, cap_sem,
):
    i = pl.program_id(0)
    start = first[tile[i]]
    stop = first[tile[i] + 1]

    def loads(b):
        span = pl.ds(pl.multiple_of(b * TB, TB), TB)
        return (
            pltpu.make_async_copy(delta_hbm.at[span], delta_v.at[span], delta_sem.at[b]),
            pltpu.make_async_copy(cap_hbm.at[span], cap_v.at[span], cap_sem.at[b]),
        )

    @pl.when(i == 0)
    def _():
        def clear(b, carry):
            state[b] = 0
            return carry

        def begin(t, carry):
            b = order[t] // KS

            @pl.when(state[b] == 0)
            def _():
                for copy in loads(b):
                    copy.start()
                state[b] = 1

            return carry

        lax.fori_loop(0, state.shape[0], clear, 0)
        lax.fori_loop(0, order.shape[0], begin, 0)

    def tiles(t):
        s = order[t]
        b = s // KS

        @pl.when(state[b] == 1)
        def _():
            for copy in loads(b):
                copy.wait()
            state[b] = 2

        tokens = pl.ds(pl.multiple_of(b * TB, TB), TB)
        mine = pl.ds(pl.multiple_of(s * TB, TB), TB)
        return (
            dot(codes_ref[mine], delta_v[tokens], 0, 0),
            dot(cap_v[tokens], dpre_ref[mine], 0, 0),
        )

    @pl.when(stop == start)
    def _():
        dec_ref[...] = jnp.zeros(dec_ref.shape, BF16)
        enc_ref[...] = jnp.zeros(enc_ref.shape, BF16)

    @pl.when(stop == start + 1)
    def _():
        d, e = tiles(start)
        dec_ref[...] = d.astype(BF16)
        enc_ref[...] = e.astype(BF16)

    @pl.when(stop > start + 1)
    def _():
        dec_acc[...], enc_acc[...] = tiles(start)

        def add(t, carry):
            d, e = tiles(t)
            dec_acc[...] += d
            enc_acc[...] += e
            return carry

        lax.fori_loop(start + 1, stop, add, 0)
        dec_ref[...] = dec_acc[...].astype(BF16)
        enc_ref[...] = enc_acc[...].astype(BF16)


def gradients(order, tile, first, delta, codes, captured, dpre):
    tokens, features = delta.shape
    blocks = tokens // TB
    groups = tile.shape[0]
    whole = pl.BlockSpec(memory_space=VMEM)
    outside = pl.BlockSpec(memory_space=pltpu.HBM)
    return pl.pallas_call(
        grads_kernel,
        grid_spec=pltpu.PrefetchScalarGridSpec(
            num_scalar_prefetch=3,
            grid=(groups,),
            in_specs=[outside, whole, outside, whole],
            out_specs=[
                pl.BlockSpec((features, LB), lambda i, order, tile, first: (0, tile[i])),
                pl.BlockSpec((LB, features), lambda i, order, tile, first: (tile[i], 0)),
            ],
            scratch_shapes=[
                VMEM((tokens, features), BF16), VMEM((tokens, features), BF16),
                VMEM((LB, features), F32), VMEM((features, LB), F32),
                pltpu.SMEM((blocks,), jnp.int32),
                pltpu.SemaphoreType.DMA((blocks,)), pltpu.SemaphoreType.DMA((blocks,)),
            ],
        ),
        out_shape=[
            jax.ShapeDtypeStruct((features, groups * LB), BF16),
            jax.ShapeDtypeStruct((groups * LB, features), BF16),
        ],
        compiler_params=pltpu.CompilerParams(vmem_limit_bytes=BIG),
        name="gradients",
    )(order, tile, first, delta, codes, captured, dpre)


def local(captured, enc_weight, enc_bias, dec_weight, dec_bias, block_ids, block_counts):
    ids = block_ids.reshape(-1)
    counts = block_counts.reshape(-1)
    pre, bias, live, order, tile, first = partial_pre(ids, counts, captured, enc_weight, enc_bias)
    codes, dpre, delta = middle(ids, pre, bias, live, dec_bias, captured, dec_weight, 16, 4)
    codes, dpre = codes.reshape(-1, LB), dpre.reshape(-1, LB)
    return tuple(gradients(order, tile, first, delta, codes, captured, dpre))


def solution(mesh):
    in_specs = (
        P(None, "tok"),
        P("tok", "lat"),
        P("lat"),
        P("lat", "tok"),
        P("tok"),
        P(None, "lat", None),
        P(None, "lat"),
    )
    out_specs = (P("tok", "lat"), P("lat", "tok"))
    return jax.shard_map(local, mesh=mesh, in_specs=in_specs, out_specs=out_specs, check_vma=False)
```
